32 devices in a mesh: groups: 2 (over x), tm: 16 (over z, y, core).
Axes of the slice: x: 2, y: 2, z: 4, core: 2. Of those that a mesh axis runs over, the one named last changes fastest.
Arguments:
- strain: bfloat16 [256, 48, 12032], P(('groups', 'tm')), parts along dimension 0
- bin_labels: int32 [256, 3], P(('groups', 'tm')), parts along dimension 0, may hold values from 0 to 7, as said below
- influence: bfloat16 [2048, 48], replicated, may hold values from -0.875 to 0.875
Outputs:
- damage_by_bin: float32 [256, 2048], P('groups', 'tm'), parts along dimension 0
- total_damage: float32 [4096], P(('groups', 'tm')), parts along dimension 0
The draws below stay inside these ranges and needn't reach their ends.
There are 2 independent parts, one for each index of `groups`. The reference program is written for one: setup_inputs(seed, part) draws one part's arguments, and reference() takes and returns one part's arrays. A program takes and returns all parts, laid end to end along the dimension named above; an argument that names none is the same for every part. Nothing has to cross between parts.
Inputs may be any that keep to these rules, and one draw needn't show every extreme that they name: `bin_labels`: columns are wind speed (below 8), direction (below 8) and yaw (below 2); every combination of the three is named by at least one block.
All inputs are finite; a program needn't handle non-finite values.
Results may differ from the reference program's by a relative error of at most 0.00059.
Values may be sent and summed in bfloat16 or wider, within the bound.
No kernel may reach another device: no remote copies, remote signals or barrier semaphores. Data moves between devices by JAX's collectives and lax.ppermute only.
A program may use at most 128 MiB of HBM per device.

```python
import math
import jax
import jax.numpy as jnp
from jax import lax

CH = 48
HOT = 2048
SEGLEN = 128
NSEG = 187
NDIR = 8
NYAW = 2
F = 64
SAMP = 12032
NBIN = 128
BLK = 128


def draw_strain(key, part):
    sub_keys = jax.random.split(key, 8)
    block_scale = jnp.exp(jax.random.uniform(sub_keys[0], (BLK, 1, 1), jnp.float32, math.log(0.25), math.log(1.25)))
    floor_slope = jax.random.uniform(sub_keys[1], (BLK, 1, 1), jnp.float32, -0.6, 0.6)
    raw_noise = jax.random.normal(sub_keys[2], (BLK, CH, SAMP + 1), jnp.float32)
    floor_part = raw_noise[:, :, 1:] + floor_slope * raw_noise[:, :, :-1]
    sample_index = jnp.arange(SAMP, dtype=jnp.int32)[None, None, :]
    modulus = 65536
    tone_sum = jnp.zeros((BLK, CH, SAMP), jnp.float32)
    peak_ranges = ((1311, 5243), (5243, 19661))
    for peak_number in range(2):
        peak_keys = jax.random.split(sub_keys[4 + peak_number], 4)
        lowest = peak_ranges[peak_number][0]
        highest = peak_ranges[peak_number][1]
        centre = jax.random.randint(peak_keys[0], (BLK, 1, 1), lowest, highest, dtype=jnp.int32)
        width_step = centre * jax.random.randint(peak_keys[1], (BLK, 1, 1), 2, 9, dtype=jnp.int32) // 100
        peak_level = jnp.exp(jax.random.uniform(peak_keys[2], (BLK, 1, 1), jnp.float32, math.log(0.25), math.log(0.8)))
        amplitude = jax.random.normal(peak_keys[3], (BLK, CH, 1), jnp.float32) * peak_level
        offset_keys = jax.random.split(sub_keys[6 + peak_number], 3)
        for tone_offset in range(3):
            tone_freq = centre + (tone_offset - 1) * width_step
            start_phase = jax.random.randint(offset_keys[tone_offset], (BLK, CH, 1), 0, modulus, dtype=jnp.int32)
            phase_index = (sample_index * tone_freq + start_phase) % modulus
            tone_sum = tone_sum + amplitude * jnp.sin(phase_index.astype(jnp.float32) * (2.0 * math.pi / modulus))
    values = (floor_part + tone_sum) * block_scale
    return values.astype(jnp.bfloat16)


def draw_bin_labels(key, part):
    key_order, key_first, key_second, key_names = jax.random.split(key, 4)
    slot_index = jnp.arange(BLK, dtype=jnp.int32)
    first_pick = jax.random.randint(key_first, (BLK,), 0, NBIN, dtype=jnp.int32)
    second_pick = jax.random.randint(key_second, (BLK,), 0, NBIN, dtype=jnp.int32)
    slot_bin = jnp.where(slot_index < NBIN, slot_index, jnp.minimum(first_pick, second_pick))
    slot_order = jax.random.permutation(key_order, BLK)
    relabel = jax.random.permutation(key_names, NBIN)
    bin_index = relabel[slot_bin[slot_order]]
    return jnp.stack([bin_index // (NDIR * NYAW), bin_index // NYAW % NDIR, bin_index % NYAW], axis=1).astype(jnp.int32)


def normal_values(key, shape, width, reach, kind=jnp.bfloat16):
    return jnp.clip(width * jax.random.normal(key, shape, jnp.float32), -reach, reach).astype(kind)


def setup_inputs(seed: int = 0, part: int = 0) -> dict:
    splits = jax.random.split(jax.random.key(seed), 4)
    part_splits = jax.random.split(jax.random.fold_in(splits[3], part), 4)
    return {
        "strain": draw_strain(jax.random.fold_in(jax.random.fold_in(splits[3], part), 71), part),
        "bin_labels": draw_bin_labels(jax.random.fold_in(jax.random.fold_in(splits[3], part), 71), part),
        "influence": normal_values(splits[2], (HOT, CH), CH ** -0.5, 0.875),
    }


def build_table():
    positions = jnp.arange(SEGLEN, dtype=jnp.int32)
    harmonic = jnp.arange(1, SEGLEN // 2 + 1, dtype=jnp.int32)
    phase = (positions[:, None] * harmonic[None, :] % SEGLEN).astype(jnp.float32) * (2.0 * math.pi / SEGLEN)
    window = 0.5 - 0.5 * jnp.cos(positions.astype(jnp.float32) * (2.0 * math.pi / SEGLEN))
    full_table = jnp.concatenate([window[:, None] * jnp.cos(phase), window[:, None] * jnp.sin(phase)], axis=1).astype(jnp.bfloat16)
    half_len = SEGLEN // 2
    return jnp.concatenate([full_table[:half_len], full_table[half_len:]], axis=1)

def block_spectra(one_block, dft_table):
    channels = one_block.shape[0]
    half_len = SEGLEN // 2
    pieces = one_block.reshape(channels * (NSEG + 1), half_len)
    product = jnp.dot(pieces, dft_table, preferred_element_type=jnp.float32).reshape(channels, NSEG + 1, 2 * SEGLEN)
    segments = (product[:, :-1, :SEGLEN] + product[:, 1:, SEGLEN:]).astype(jnp.bfloat16)
    ordered = jnp.transpose(segments, (2, 0, 1)).astype(jnp.float32)
    cross = jnp.einsum('gcs,gds->gcd', ordered, ordered)
    cospec = (cross[:half_len] + cross[half_len:]) * (8.0 / (3.0 * SEGLEN * NSEG))
    return cospec.reshape(-1).astype(jnp.bfloat16)

def spectral_moments(stress, frequency):
    moment_zero = lax.optimization_barrier(jnp.sum(stress, axis=0)) / SEGLEN
    moment_one = lax.optimization_barrier(jnp.sum(frequency[:, None] * stress, axis=0)) / SEGLEN
    moment_two = lax.optimization_barrier(jnp.sum(frequency[:, None] ** 2 * stress, axis=0)) / SEGLEN
    moment_four = lax.optimization_barrier(jnp.sum(frequency[:, None] ** 4 * stress, axis=0)) / SEGLEN
    return jnp.stack([moment_zero, moment_one, moment_two, moment_four], axis=0)

def dirlik(moment_zero, moment_one, moment_two, moment_four):
    spread_ratio = moment_two / jnp.sqrt(moment_zero * moment_four)
    mean_freq = moment_one / moment_zero * jnp.sqrt(moment_two / moment_four)
    d_one = 2.0 * (mean_freq - spread_ratio ** 2) / (1.0 + spread_ratio ** 2)
    shared = 1.0 - spread_ratio - d_one + d_one ** 2
    r_ratio = (spread_ratio - mean_freq - d_one ** 2) / shared
    d_two = shared / (1.0 - r_ratio)
    d_three = 1.0 - d_one - d_two
    q_factor = 1.25 * (spread_ratio - d_three - d_two * r_ratio) / d_one
    peak_rate = jnp.sqrt(moment_four / moment_two)
    bracket = 6.0 * d_one * q_factor ** 3 + 2.8284271247 * 1.3293403882 * (jnp.abs(r_ratio) ** 3 * d_two + d_three)
    return peak_rate * (2.0 * jnp.sqrt(moment_zero)) ** 3 * bracket

def reference(strain, bin_labels, influence):
    dft_table = build_table()
    cospec = lax.map(lambda one_block: block_spectra(one_block, dft_table), strain)
    bin_index = (bin_labels[:, 0] * NDIR + bin_labels[:, 1]) * NYAW + bin_labels[:, 2]
    onehot = (bin_index[None, :] == jnp.arange(NBIN, dtype=jnp.int32)[:, None]).astype(jnp.bfloat16)
    count = lax.optimization_barrier(jnp.sum(onehot.astype(jnp.float32), axis=1))
    bin_sums = jnp.dot(onehot, cospec, preferred_element_type=jnp.float32)
    mean_cospec = bin_sums / count[:, None]
    weights_f32 = influence.astype(jnp.float32)
    frequency = jnp.arange(1, F + 1, dtype=jnp.int32).astype(jnp.float32) / SEGLEN

    def bin_damage(flat_mean):
        product = jnp.dot(flat_mean.reshape(F * CH, CH), weights_f32.T, precision=lax.Precision.HIGHEST)
        stress = lax.optimization_barrier(jnp.sum(product.reshape(F, CH, HOT) * weights_f32.T[None], axis=1))
        moments = spectral_moments(stress, frequency)
        return dirlik(moments[0], moments[1], moments[2], moments[3])
    damage_by_bin = lax.map(bin_damage, mean_cospec)
    total_damage = lax.optimization_barrier(jnp.sum(count[:, None] / BLK * damage_by_bin, axis=0))
    return (damage_by_bin, total_damage)
```

```python
import functools
import math

import jax
import jax.numpy as jnp
from jax import lax
from jax.experimental import pallas as pl
from jax.experimental.pallas import tpu as pltpu
from jax.sharding import PartitionSpec as P

SEGLEN = 128
NSEG = 187
NDIR = 8
NYAW = 2
NBIN = 128
LANES = 128
HALF = SEGLEN // 2
CPAD = 64
NMOM = 4
NT = (((1,), (1,)), ((), ()))


def build_table():
    positions = jnp.arange(SEGLEN, dtype=jnp.int32)
    harmonic = jnp.arange(1, SEGLEN // 2 + 1, dtype=jnp.int32)
    phase = (positions[:, None] * harmonic[None, :] % SEGLEN).astype(jnp.float32) * (
        2.0 * math.pi / SEGLEN
    )
    window = 0.5 - 0.5 * jnp.cos(positions.astype(jnp.float32) * (2.0 * math.pi / SEGLEN))
    return jnp.concatenate(
        [window[:, None] * jnp.cos(phase), window[:, None] * jnp.sin(phase)], axis=1
    ).astype(jnp.bfloat16)


def pair_table():
    columns = build_table().T
    even = jnp.pad(columns, ((0, 0), (0, SEGLEN)))
    odd = jnp.pad(columns, ((0, 0), (HALF, HALF)))
    return jnp.concatenate([even, odd], axis=0)


def split3(value):
    high = value.astype(jnp.bfloat16)
    rest = value - high.astype(jnp.float32)
    middle = rest.astype(jnp.bfloat16)
    low = (rest - middle.astype(jnp.float32)).astype(jnp.bfloat16)
    return high, middle, low


def moments_kernel(
    blocks, channels, tiles, labels, strain, table, influence, out, xs, even, odd, weights, columns, parts
):
    block = pl.program_id(0)
    hotspots = influence.shape[0]
    freq_count = SEGLEN // 2
    rows = xs.shape[0] // channels

    @pl.when(block == 0)
    def _():
        xs[...] = jnp.zeros_like(xs)
        even[...] = jnp.zeros_like(even)
        odd[...] = jnp.zeros_like(odd)
        weights[...] = jnp.zeros_like(weights)
        for part in range(3):
            weights[:, part * CPAD : part * CPAD + channels] = influence[...]
        row = lax.broadcasted_iota(jnp.int32, (channels, channels), 0)
        col = lax.broadcasted_iota(jnp.int32, (channels, channels), 1)
        eye = jnp.where(row == col, 1.0, 0.0).astype(jnp.bfloat16)
        columns[...] = lax.dot_general(eye, influence[...], NT, preferred_element_type=jnp.float32)

    for tile in range(tiles):
        xs[tile * channels : (tile + 1) * channels, :] = strain[
            0, :, tile * LANES : (tile + 1) * LANES
        ].astype(jnp.float32)

    pair_rows = table[...]

    def transform(pair, carry):
        windows = []
        for offset in range(2):
            channel = 2 * pair + offset
            here = xs[pl.ds(channel, LANES, stride=channels), :].astype(jnp.bfloat16)
            after = xs[pl.ds(channel + channels, LANES, stride=channels), :].astype(jnp.bfloat16)
            windows.append(jnp.concatenate([here, after], axis=1))
        window = jnp.concatenate(windows, axis=0)
        coeffs = lax.dot_general(pair_rows, window, NT, preferred_element_type=jnp.float32)
        for offset in range(2):
            channel = 2 * pair + offset
            lanes = slice(offset * LANES, (offset + 1) * LANES)
            even[pl.ds(channel, SEGLEN, stride=CPAD), :] = coeffs[:SEGLEN, lanes]
            odd[pl.ds(channel, SEGLEN, stride=CPAD), :] = coeffs[SEGLEN:, lanes]
        return carry

    lax.fori_loop(0, channels // 2, transform, 0, unroll=2)

    lane = lax.broadcasted_iota(jnp.int32, (1, LANES), 1)
    keep_odd = lane < tiles - 1
    first_half = lane < CPAD
    scale = 8.0 / (3.0 * SEGLEN * NSEG)

    def cross(pair, totals):
        pieces = []
        for base in (0, freq_count):
            start = pl.multiple_of((base + 2 * pair) * CPAD, 2 * CPAD)
            pieces.append(even[pl.ds(start, 2 * CPAD), :].astype(jnp.bfloat16))
            pieces.append(
                jnp.where(keep_odd, odd[pl.ds(start, 2 * CPAD), :], 0.0).astype(jnp.bfloat16)
            )
        right = jnp.concatenate(pieces, axis=1)
        left = jnp.concatenate([right[:channels], right[CPAD : CPAD + channels]], axis=0)
        product = lax.dot_general(left, right, NT, preferred_element_type=jnp.float32)
        cospec = jnp.where(first_half, product[:channels], product[channels:]) * scale
        cospec = cospec.astype(jnp.bfloat16).astype(jnp.float32)
        index = 2 * pair + 1 + jnp.where(first_half, 0, 1)
        frequency = index.astype(jnp.float32) / SEGLEN
        square = frequency * frequency
        return (
            totals[0] + cospec,
            totals[1] + cospec * frequency,
            totals[2] + cospec * square,
            totals[3] + cospec * (square * square),
        )

    zero = jnp.zeros((channels, LANES), jnp.float32)
    totals = lax.fori_loop(0, freq_count // 2, cross, (zero,) * NMOM, unroll=2)
    for moment in range(NMOM):
        whole = totals[moment] + pltpu.roll(totals[moment], CPAD, 1)
        high, middle, low = split3(whole * (1.0 / SEGLEN))
        start = pl.multiple_of((moment * blocks + block) * channels, 16)
        parts[pl.ds(start, channels), :LANES] = jnp.where(first_half, high, middle)
        parts[pl.ds(start, channels), LANES:] = low

    @pl.when(block == blocks - 1)
    def _():
        width = 2 * LANES

        def project(step, carry):
            start = pl.multiple_of(step * width, width)
            spread = lax.dot_general(
                parts[...], weights[pl.ds(start, width), :], NT, preferred_element_type=jnp.float32
            )
            spread = spread.reshape(NMOM * blocks, channels, width)
            moments = jnp.sum(spread * columns[:, pl.ds(start, width)][None], axis=1)
            for half in range(2):
                for moment in range(NMOM):
                    out[2 * step + half, moment] = moments[
                        moment * blocks : (moment + 1) * blocks, half * LANES : (half + 1) * LANES
                    ]
            return carry

        lax.fori_loop(0, hotspots // width, project, 0)
        row = lax.broadcasted_iota(jnp.int32, (blocks, LANES), 0)
        named = jnp.zeros((blocks, LANES), jnp.float32)
        for index in range(blocks):
            label = (labels[index, 0] * NDIR + labels[index, 1]) * NYAW + labels[index, 2]
            named = jnp.where(row == index, label.astype(jnp.float32), named)
        for step in range(hotspots // LANES):
            out[step, NMOM] = named


def local_moments(strain, bin_labels, influence):
    blocks, channels, samples = strain.shape
    hotspots = influence.shape[0]
    tiles = samples // LANES
    table = pair_table()
    return pl.pallas_call(
        functools.partial(moments_kernel, blocks, channels, tiles),
        grid=(blocks,),
        in_specs=[
            pl.BlockSpec(memory_space=pltpu.SMEM),
            pl.BlockSpec((1, channels, samples), lambda b: (b, 0, 0)),
            pl.BlockSpec((2 * SEGLEN, 2 * SEGLEN), lambda b: (0, 0)),
            pl.BlockSpec((hotspots, channels), lambda b: (0, 0)),
        ],
        out_specs=pl.BlockSpec((hotspots // LANES, NMOM + 1, blocks, LANES), lambda b: (0, 0, 0, 0)),
        out_shape=jax.ShapeDtypeStruct((hotspots // LANES, NMOM + 1, blocks, LANES), jnp.float32),
        scratch_shapes=[
            pltpu.VMEM(((LANES + 1) * channels, LANES), jnp.float32),
            pltpu.VMEM((SEGLEN * CPAD, LANES), jnp.float32),
            pltpu.VMEM((SEGLEN * CPAD, LANES), jnp.float32),
            pltpu.VMEM((hotspots, 2 * LANES), jnp.bfloat16),
            pltpu.VMEM((channels, hotspots), jnp.float32),
            pltpu.VMEM((NMOM * blocks * channels, 2 * LANES), jnp.bfloat16),
        ],
        compiler_params=pltpu.CompilerParams(vmem_limit_bytes=48 << 20),
        name="block_moments",
    )(bin_labels, strain, table, influence)


def dirlik(moment_zero, moment_one, moment_two, moment_four):
    spread_ratio = moment_two / jnp.sqrt(moment_zero * moment_four)
    mean_freq = moment_one / moment_zero * jnp.sqrt(moment_two / moment_four)
    d_one = 2.0 * (mean_freq - spread_ratio**2) / (1.0 + spread_ratio**2)
    shared = 1.0 - spread_ratio - d_one + d_one**2
    r_ratio = (spread_ratio - mean_freq - d_one**2) / shared
    d_two = shared / (1.0 - r_ratio)
    d_three = 1.0 - d_one - d_two
    q_factor = 1.25 * (spread_ratio - d_three - d_two * r_ratio) / d_one
    peak_rate = jnp.sqrt(moment_four / moment_two)
    bracket = 6.0 * d_one * q_factor**3 + 2.8284271247 * 1.3293403882 * (
        jnp.abs(r_ratio) ** 3 * d_two + d_three
    )
    return peak_rate * (2.0 * jnp.sqrt(moment_zero)) ** 3 * bracket


def damage_kernel(received, damage, total):
    sources, _, blocks, width = received.shape
    count_blocks = sources * blocks
    named = received[:, NMOM].reshape(count_blocks, width)[:, :1]
    bins = lax.broadcasted_iota(jnp.int32, (count_blocks, NBIN), 1).astype(jnp.float32)
    member = jnp.where(named == bins, 1.0, 0.0)
    chosen = member.T.astype(jnp.bfloat16)
    count = jnp.sum(member.T, axis=1, keepdims=True)
    means = []
    for moment in range(NMOM):
        total_moment = jnp.zeros((NBIN, width), jnp.float32)
        for piece in split3(received[:, moment].reshape(count_blocks, width)):
            total_moment = total_moment + jnp.dot(chosen, piece, preferred_element_type=jnp.float32)
        means.append(total_moment / count)
    by_bin = dirlik(*means)
    damage[...] = by_bin
    total[...] = jnp.sum(count / count_blocks * by_bin, axis=0, keepdims=True)


def per_device(strain, bin_labels, influence):
    devices = lax.axis_size("tm")
    blocks = strain.shape[0]
    hotspots = influence.shape[0]
    width = hotspots // devices
    moments = local_moments(strain, bin_labels, influence)
    if width != LANES:
        share = LANES // width
        moments = moments.reshape(hotspots // LANES, NMOM + 1, blocks, share, width)
        moments = moments.transpose(0, 3, 1, 2, 4).reshape(devices, NMOM + 1, blocks, width)
    received = lax.all_to_all(moments, "tm", split_axis=0, concat_axis=0, tiled=True)
    damage, total = pl.pallas_call(
        damage_kernel,
        out_shape=(
            jax.ShapeDtypeStruct((NBIN, width), jnp.float32),
            jax.ShapeDtypeStruct((1, width), jnp.float32),
        ),
        name="bin_damage",
    )(received)
    return damage, total.reshape(width)


def solution(mesh):
    placed = (P(("groups", "tm"), None, None), P(("groups", "tm"), None), P())
    return jax.shard_map(
        per_device,
        mesh=mesh,
        in_specs=placed,
        out_specs=(P("groups", "tm"), P(("groups", "tm"))),
        check_vma=False,
    )
```

```python
import functools
import math

import jax
import jax.numpy as jnp
import ml_dtypes
import numpy as np
from jax import lax
from jax.experimental import pallas as pl
from jax.experimental.pallas import tpu as pltpu
from jax.sharding import PartitionSpec as P

SEGLEN = 128
NSEG = 187
NDIR = 8
NYAW = 2
NBIN = 128
LANES = 128
HALF = SEGLEN // 2
CPAD = 64
NMOM = 4
NT = (((1,), (1,)), ((), ()))


def build_table():
    positions = np.arange(SEGLEN)
    harmonic = np.arange(1, SEGLEN // 2 + 1)
    phase = (positions[:, None] * harmonic[None, :] % SEGLEN) * (2.0 * math.pi / SEGLEN)
    window = 0.5 - 0.5 * np.cos(positions * (2.0 * math.pi / SEGLEN))
    table = np.concatenate([window[:, None] * np.cos(phase), window[:, None] * np.sin(phase)], axis=1)
    return table.astype(ml_dtypes.bfloat16)


def pair_table():
    columns = build_table().T
    even = np.pad(columns, ((0, 0), (0, SEGLEN)))
    odd = np.pad(columns, ((0, 0), (HALF, HALF)))
    return np.concatenate([even, odd], axis=0)


def split3(value):
    high = value.astype(jnp.bfloat16)
    rest = value - high.astype(jnp.float32)
    middle = rest.astype(jnp.bfloat16)
    low = (rest - middle.astype(jnp.float32)).astype(jnp.bfloat16)
    return high, middle, low


def moments_kernel(
    blocks, channels, tiles, labels, strain, table, influence, out, xs, even, odd, weights, parts
):
    block = pl.program_id(0)
    hotspots = influence.shape[1]
    freq_count = SEGLEN // 2

    @pl.when(block == 0)
    def _():
        xs[tiles * channels :, :] = jnp.zeros((xs.shape[0] - tiles * channels, LANES), jnp.float32)
        weights[...] = jnp.zeros_like(weights)
        for part in range(3):
            weights[part * CPAD : part * CPAD + channels, :] = influence[...]

    for tile in range(tiles):
        xs[tile * channels : (tile + 1) * channels, :] = strain[
            0, :, tile * LANES : (tile + 1) * LANES
        ].astype(jnp.float32)

    pair_rows = table[...]
    for pair in range(channels // 2):
        windows = []
        for channel in (2 * pair, 2 * pair + 1):
            here = xs[pl.ds(channel, LANES, stride=channels), :].astype(jnp.bfloat16)
            after = xs[pl.ds(channel + channels, LANES, stride=channels), :].astype(jnp.bfloat16)
            windows.append(jnp.concatenate([here, after], axis=1))
        window = jnp.concatenate(windows, axis=0)
        coeffs = lax.dot_general(pair_rows, window, NT, preferred_element_type=jnp.float32)
        for offset in range(2):
            channel = 2 * pair + offset
            lanes = slice(offset * LANES, (offset + 1) * LANES)
            even[pl.ds(channel, SEGLEN, stride=channels), :] = coeffs[:SEGLEN, lanes]
            odd[pl.ds(channel, SEGLEN, stride=channels), :] = coeffs[SEGLEN:, lanes]

    lane = lax.broadcasted_iota(jnp.int32, (1, LANES), 1)
    keep_odd = lane < tiles - 1
    first_half = lane < CPAD
    half_index = jnp.where(first_half, 1, 2).astype(jnp.float32)
    scale = 8.0 / (3.0 * SEGLEN * NSEG)
    totals = [jnp.zeros((channels, LANES), jnp.float32)] * NMOM
    gap = jnp.zeros((CPAD - channels, 4 * LANES), jnp.bfloat16)
    for pair in range(freq_count // 2):
        sides = []
        for freq in (2 * pair, 2 * pair + 1):
            pieces = []
            for line in (freq, freq + freq_count):
                rows = slice(line * channels, (line + 1) * channels)
                pieces.append(even[rows, :].astype(jnp.bfloat16))
                pieces.append(jnp.where(keep_odd, odd[rows, :], 0.0).astype(jnp.bfloat16))
            sides.append(jnp.concatenate(pieces, axis=1))
        left = jnp.concatenate(sides, axis=0)
        right = jnp.concatenate([sides[0], gap, sides[1], gap], axis=0)
        product = lax.dot_general(left, right, NT, preferred_element_type=jnp.float32)
        cospec = jnp.where(first_half, product[:channels], product[channels:]) * scale
        cospec = cospec.astype(jnp.bfloat16).astype(jnp.float32)
        frequency = (half_index + 2.0 * pair) * (1.0 / SEGLEN)
        square = frequency * frequency
        totals[0] = totals[0] + cospec
        totals[1] = totals[1] + cospec * frequency
        totals[2] = totals[2] + cospec * square
        totals[3] = totals[3] + cospec * (square * square)

    for moment in range(NMOM):
        whole = totals[moment] + pltpu.roll(totals[moment], CPAD, 1)
        high, middle, low = split3(whole * (1.0 / SEGLEN))
        start = pl.multiple_of((moment * blocks + block) * channels, 16)
        parts[pl.ds(start, channels), :LANES] = jnp.where(first_half, high, middle)
        parts[pl.ds(start, channels), LANES:] = low

    @pl.when(block == blocks - 1)
    def _():
        width = 2 * LANES
        for step in range(hotspots // width):
            lanes = slice(step * width, (step + 1) * width)
            column = influence[:, lanes].astype(jnp.float32)
            for moment in range(NMOM):
                rows = slice(moment * blocks * channels, (moment + 1) * blocks * channels)
                spread = jnp.dot(parts[rows, :], weights[:, lanes], preferred_element_type=jnp.float32)
                spread = spread.reshape(blocks, channels, width)
                value = jnp.sum(spread * column[None], axis=1)
                for half in range(2):
                    out[2 * step + half, moment] = value[:, half * LANES : (half + 1) * LANES]
        row = lax.broadcasted_iota(jnp.int32, (blocks, LANES), 0)
        named = jnp.zeros((blocks, LANES), jnp.float32)
        for index in range(blocks):
            label = (labels[0, index] * NDIR + labels[1, index]) * NYAW + labels[2, index]
            named = jnp.where(row == index, label.astype(jnp.float32), named)
        for step in range(hotspots // LANES):
            out[step, NMOM] = named


def local_moments(strain, bin_labels, influence):
    blocks, channels, samples = strain.shape
    hotspots = influence.shape[0]
    tiles = samples // LANES
    return pl.pallas_call(
        functools.partial(moments_kernel, blocks, channels, tiles),
        grid=(blocks,),
        in_specs=[
            pl.BlockSpec(memory_space=pltpu.SMEM),
            pl.BlockSpec((1, channels, samples), lambda b: (b, 0, 0)),
            pl.BlockSpec((2 * SEGLEN, 2 * SEGLEN), lambda b: (0, 0)),
            pl.BlockSpec((channels, hotspots), lambda b: (0, 0)),
        ],
        out_specs=pl.BlockSpec((hotspots // LANES, NMOM + 1, blocks, LANES), lambda b: (0, 0, 0, 0)),
        out_shape=jax.ShapeDtypeStruct((hotspots // LANES, NMOM + 1, blocks, LANES), jnp.float32),
        scratch_shapes=[
            pltpu.VMEM(((LANES + 1) * channels, LANES), jnp.float32),
            pltpu.VMEM((SEGLEN * channels, LANES), jnp.float32),
            pltpu.VMEM((SEGLEN * channels, LANES), jnp.float32),
            pltpu.VMEM((2 * LANES, hotspots), jnp.bfloat16),
            pltpu.VMEM((NMOM * blocks * channels, 2 * LANES), jnp.bfloat16),
        ],
        compiler_params=pltpu.CompilerParams(vmem_limit_bytes=48 << 20),
        name="block_moments",
    )(bin_labels.T, strain, jnp.asarray(pair_table()), influence.T)


def dirlik(moment_zero, moment_one, moment_two, moment_four):
    spread_ratio = moment_two / jnp.sqrt(moment_zero * moment_four)
    mean_freq = moment_one / moment_zero * jnp.sqrt(moment_two / moment_four)
    d_one = 2.0 * (mean_freq - spread_ratio**2) / (1.0 + spread_ratio**2)
    shared = 1.0 - spread_ratio - d_one + d_one**2
    r_ratio = (spread_ratio - mean_freq - d_one**2) / shared
    d_two = shared / (1.0 - r_ratio)
    d_three = 1.0 - d_one - d_two
    q_factor = 1.25 * (spread_ratio - d_three - d_two * r_ratio) / d_one
    peak_rate = jnp.sqrt(moment_four / moment_two)
    bracket = 6.0 * d_one * q_factor**3 + 2.8284271247 * 1.3293403882 * (
        jnp.abs(r_ratio) ** 3 * d_two + d_three
    )
    return peak_rate * (2.0 * jnp.sqrt(moment_zero)) ** 3 * bracket


def damage_kernel(received, damage, total):
    sources, _, blocks, width = received.shape
    count_blocks = sources * blocks
    named = received[:, NMOM].reshape(count_blocks, width)[:, :1]
    bins = lax.broadcasted_iota(jnp.int32, (count_blocks, NBIN), 1).astype(jnp.float32)
    member = jnp.where(named == bins, 1.0, 0.0)
    chosen = member.T.astype(jnp.bfloat16)
    count = jnp.sum(member.T, axis=1, keepdims=True)
    means = []
    for moment in range(NMOM):
        total_moment = jnp.zeros((NBIN, width), jnp.float32)
        for piece in split3(received[:, moment].reshape(count_blocks, width)):
            total_moment = total_moment + jnp.dot(chosen, piece, preferred_element_type=jnp.float32)
        means.append(total_moment / count)
    by_bin = dirlik(*means)
    damage[...] = by_bin
    total[...] = jnp.sum(count / count_blocks * by_bin, axis=0, keepdims=True)


def per_device(strain, bin_labels, influence):
    devices = lax.axis_size("tm")
    blocks = strain.shape[0]
    hotspots = influence.shape[0]
    width = hotspots // devices
    moments = local_moments(strain, bin_labels, influence)
    if width != LANES:
        share = LANES // width
        moments = moments.reshape(hotspots // LANES, NMOM + 1, blocks, share, width)
        moments = moments.transpose(0, 3, 1, 2, 4).reshape(devices, NMOM + 1, blocks, width)
    received = lax.all_to_all(moments, "tm", split_axis=0, concat_axis=0, tiled=True)
    damage, total = pl.pallas_call(
        damage_kernel,
        out_shape=(
            jax.ShapeDtypeStruct((NBIN, width), jnp.float32),
            jax.ShapeDtypeStruct((1, width), jnp.float32),
        ),
        name="bin_damage",
    )(received)
    return damage, total.reshape(width)


def solution(mesh):
    placed = (P(("groups", "tm"), None, None), P(("groups", "tm"), None), P())
    return jax.shard_map(
        per_device,
        mesh=mesh,
        in_specs=placed,
        out_specs=(P("groups", "tm"), P(("groups", "tm"))),
        check_vma=False,
    )
```

```python
import functools
import math

import jax
import jax.numpy as jnp
import ml_dtypes
import numpy as np
from jax import lax
from jax.experimental import pallas as pl
from jax.experimental.pallas import tpu as pltpu
from jax.sharding import PartitionSpec as P

SEGLEN = 128
NSEG = 187
NDIR = 8
NYAW = 2
NBIN = 128
LANES = 128
HALF = SEGLEN // 2
CPAD = 64
NMOM = 4
WINDOWS = 96
STRIDE = 49
NT = (((1,), (1,)), ((), ()))


def build_table():
    positions = np.arange(SEGLEN)
    harmonic = np.arange(1, SEGLEN // 2 + 1)
    phase = (positions[:, None] * harmonic[None, :] % SEGLEN) * (2.0 * math.pi / SEGLEN)
    window = 0.5 - 0.5 * np.cos(positions * (2.0 * math.pi / SEGLEN))
    table = np.concatenate([window[:, None] * np.cos(phase), window[:, None] * np.sin(phase)], axis=1)
    return table.astype(ml_dtypes.bfloat16)


def pair_table():
    columns = build_table().T
    even = np.pad(columns, ((0, 0), (0, SEGLEN)))
    odd = np.pad(columns, ((0, 0), (HALF, HALF)))
    return np.concatenate([even, odd], axis=0)


def split3(value):
    high = value.astype(jnp.bfloat16)
    rest = value - high.astype(jnp.float32)
    middle = rest.astype(jnp.bfloat16)
    low = (rest - middle.astype(jnp.float32)).astype(jnp.bfloat16)
    return high, middle, low


def moments_kernel(
    blocks, channels, tiles, labels, strain, table, influence, out, xs, even, odd, weights, parts
):
    block = pl.program_id(0)
    hotspots = influence.shape[1]
    freq_count = SEGLEN // 2

    @pl.when(block == 0)
    def _():
        xs[tiles * STRIDE :, :] = jnp.zeros((xs.shape[0] - tiles * STRIDE, LANES), jnp.float32)
        weights[...] = jnp.zeros_like(weights)
        for part in range(3):
            weights[part * CPAD : part * CPAD + channels, :] = influence[...]

    for tile in range(tiles):
        xs[tile * STRIDE : tile * STRIDE + channels, :] = strain[
            0, :, tile * LANES : (tile + 1) * LANES
        ].astype(jnp.float32)

    pair_rows = table[...]
    spare = jnp.zeros((LANES - WINDOWS, 2 * LANES), jnp.bfloat16)
    for pair in range(channels // 2):
        windows = []
        for channel in (2 * pair, 2 * pair + 1):
            here = xs[pl.ds(channel, WINDOWS, stride=STRIDE), :].astype(jnp.bfloat16)
            after = xs[pl.ds(channel + STRIDE, WINDOWS, stride=STRIDE), :].astype(jnp.bfloat16)
            windows += [jnp.concatenate([here, after], axis=1), spare]
        window = jnp.concatenate(windows, axis=0)
        coeffs = lax.dot_general(pair_rows, window, NT, preferred_element_type=jnp.float32)
        for offset in range(2):
            channel = 2 * pair + offset
            lanes = slice(offset * LANES, (offset + 1) * LANES)
            even[pl.ds(channel, SEGLEN, stride=STRIDE), :] = coeffs[:SEGLEN, lanes]
            odd[pl.ds(channel, SEGLEN, stride=STRIDE), :] = coeffs[SEGLEN:, lanes]

    lane = lax.broadcasted_iota(jnp.int32, (1, LANES), 1)
    keep_odd = lane < tiles - 1
    first_half = lane[:, : 2 * channels] < channels
    half_index = jnp.where(first_half, 1, 2).astype(jnp.float32)
    scale = 8.0 / (3.0 * SEGLEN * NSEG)

    totals = [jnp.zeros((channels, 2 * channels), jnp.float32)] * NMOM
    for pair in range(freq_count // 2):
        sides = []
        for freq in (2 * pair, 2 * pair + 1):
            pieces = []
            for line in (freq, freq + freq_count):
                rows = slice(line * STRIDE, line * STRIDE + channels)
                pieces.append(even[rows, :].astype(jnp.bfloat16))
                pieces.append(jnp.where(keep_odd, odd[rows, :].astype(jnp.bfloat16), jnp.bfloat16(0)))
            sides.append(jnp.concatenate(pieces, axis=1))
        both = jnp.concatenate(sides, axis=0)
        product = lax.dot_general(both, both, NT, preferred_element_type=jnp.float32)
        cospec = jnp.where(first_half, product[:channels], product[channels:]) * scale
        cospec = cospec.astype(jnp.bfloat16).astype(jnp.float32)
        frequency = (half_index + 2.0 * pair) * (1.0 / SEGLEN)
        square = frequency * frequency
        totals[0] = totals[0] + cospec
        totals[1] = totals[1] + cospec * frequency
        totals[2] = totals[2] + cospec * square
        totals[3] = totals[3] + cospec * (square * square)

    for moment in range(NMOM):
        whole = (totals[moment][:, :channels] + totals[moment][:, channels:]) * (1.0 / SEGLEN)
        whole = jnp.concatenate([whole, jnp.zeros((channels, CPAD - channels), jnp.float32)] * 2, axis=1)
        high, middle, low = split3(whole)
        start = pl.multiple_of((moment * blocks + block) * channels, 16)
        parts[pl.ds(start, channels), :LANES] = jnp.where(lane < CPAD, high, middle)
        parts[pl.ds(start, channels), LANES:] = low

    @pl.when(block == blocks - 1)
    def _():
        width = 2 * LANES
        for step in range(hotspots // width):
            lanes = slice(step * width, (step + 1) * width)
            column = influence[:, lanes].astype(jnp.float32)
            for moment in range(NMOM):
                rows = slice(moment * blocks * channels, (moment + 1) * blocks * channels)
                spread = jnp.dot(parts[rows, :], weights[:, lanes], preferred_element_type=jnp.float32)
                spread = spread.reshape(blocks, channels, width)
                value = jnp.sum(spread * column[None], axis=1)
                for half in range(2):
                    out[2 * step + half, moment] = value[:, half * LANES : (half + 1) * LANES]
        row = lax.broadcasted_iota(jnp.int32, (blocks, LANES), 0)
        named = jnp.zeros((blocks, LANES), jnp.float32)
        for index in range(blocks):
            label = (labels[0, index] * NDIR + labels[1, index]) * NYAW + labels[2, index]
            named = jnp.where(row == index, label.astype(jnp.float32), named)
        for step in range(hotspots // LANES):
            out[step, NMOM] = named


def local_moments(strain, bin_labels, influence):
    blocks, channels, samples = strain.shape
    hotspots = influence.shape[0]
    tiles = samples // LANES
    return pl.pallas_call(
        functools.partial(moments_kernel, blocks, channels, tiles),
        grid=(blocks,),
        in_specs=[
            pl.BlockSpec(memory_space=pltpu.SMEM),
            pl.BlockSpec((1, channels, samples), lambda b: (b, 0, 0)),
            pl.BlockSpec((2 * SEGLEN, 2 * SEGLEN), lambda b: (0, 0)),
            pl.BlockSpec((channels, hotspots), lambda b: (0, 0)),
        ],
        out_specs=pl.BlockSpec((hotspots // LANES, NMOM + 1, blocks, LANES), lambda b: (0, 0, 0, 0)),
        out_shape=jax.ShapeDtypeStruct((hotspots // LANES, NMOM + 1, blocks, LANES), jnp.float32),
        scratch_shapes=[
            pltpu.VMEM(((LANES + 1) * STRIDE, LANES), jnp.float32),
            pltpu.VMEM((SEGLEN * STRIDE, LANES), jnp.float32),
            pltpu.VMEM((SEGLEN * STRIDE, LANES), jnp.float32),
            pltpu.VMEM((2 * LANES, hotspots), jnp.bfloat16),
            pltpu.VMEM((NMOM * blocks * channels, 2 * LANES), jnp.bfloat16),
        ],
        compiler_params=pltpu.CompilerParams(vmem_limit_bytes=60 << 20),
        name="block_moments",
    )(bin_labels.T, strain, jnp.asarray(pair_table()), influence.T)


def dirlik(moment_zero, moment_one, moment_two, moment_four):
    spread_ratio = moment_two / jnp.sqrt(moment_zero * moment_four)
    mean_freq = moment_one / moment_zero * jnp.sqrt(moment_two / moment_four)
    d_one = 2.0 * (mean_freq - spread_ratio**2) / (1.0 + spread_ratio**2)
    shared = 1.0 - spread_ratio - d_one + d_one**2
    r_ratio = (spread_ratio - mean_freq - d_one**2) / shared
    d_two = shared / (1.0 - r_ratio)
    d_three = 1.0 - d_one - d_two
    q_factor = 1.25 * (spread_ratio - d_three - d_two * r_ratio) / d_one
    peak_rate = jnp.sqrt(moment_four / moment_two)
    bracket = 6.0 * d_one * q_factor**3 + 2.8284271247 * 1.3293403882 * (
        jnp.abs(r_ratio) ** 3 * d_two + d_three
    )
    return peak_rate * (2.0 * jnp.sqrt(moment_zero)) ** 3 * bracket


def damage_kernel(received, damage, total):
    sources, _, blocks, width = received.shape
    count_blocks = sources * blocks
    named = received[:, NMOM].reshape(count_blocks, width)[:, :1]
    bins = lax.broadcasted_iota(jnp.int32, (count_blocks, NBIN), 1).astype(jnp.float32)
    member = jnp.where(named == bins, 1.0, 0.0)
    chosen = member.T.astype(jnp.bfloat16)
    count = jnp.sum(member.T, axis=1, keepdims=True)
    means = []
    for moment in range(NMOM):
        total_moment = jnp.zeros((NBIN, width), jnp.float32)
        for piece in split3(received[:, moment].reshape(count_blocks, width)):
            total_moment = total_moment + jnp.dot(chosen, piece, preferred_element_type=jnp.float32)
        means.append(total_moment / count)
    by_bin = dirlik(*means)
    damage[...] = by_bin
    total[...] = jnp.sum(count / count_blocks * by_bin, axis=0, keepdims=True)


def per_device(strain, bin_labels, influence):
    devices = lax.axis_size("tm")
    blocks = strain.shape[0]
    hotspots = influence.shape[0]
    width = hotspots // devices
    moments = local_moments(strain, bin_labels, influence)
    if width != LANES:
        share = LANES // width
        moments = moments.reshape(hotspots // LANES, NMOM + 1, blocks, share, width)
        moments = moments.transpose(0, 3, 1, 2, 4).reshape(devices, NMOM + 1, blocks, width)
    received = lax.all_to_all(moments, "tm", split_axis=0, concat_axis=0, tiled=True)
    damage, total = pl.pallas_call(
        damage_kernel,
        out_shape=(
            jax.ShapeDtypeStruct((NBIN, width), jnp.float32),
            jax.ShapeDtypeStruct((1, width), jnp.float32),
        ),
        name="bin_damage",
    )(received)
    return damage, total.reshape(width)


def solution(mesh):
    placed = (P(("groups", "tm"), None, None), P(("groups", "tm"), None), P())
    return jax.shard_map(
        per_device,
        mesh=mesh,
        in_specs=placed,
        out_specs=(P("groups", "tm"), P(("groups", "tm"))),
        check_vma=False,
    )
```

```python
import functools
import math

import jax
import jax.numpy as jnp
import ml_dtypes
import numpy as np
from jax import lax
from jax.experimental import pallas as pl
from jax.experimental.pallas import tpu as pltpu
from jax.sharding import PartitionSpec as P

SEGLEN = 128
NSEG = 187
NDIR = 8
NYAW = 2
NBIN = 128
LANES = 128
HALF = SEGLEN // 2
CPAD = 64
NMOM = 4
WINDOWS = 96
STRIDE = 49
NT = (((1,), (1,)), ((), ()))


def build_table():
    positions = np.arange(SEGLEN)
    harmonic = np.arange(1, SEGLEN // 2 + 1)
    phase = (positions[:, None] * harmonic[None, :] % SEGLEN) * (2.0 * math.pi / SEGLEN)
    window = 0.5 - 0.5 * np.cos(positions * (2.0 * math.pi / SEGLEN))
    table = np.concatenate([window[:, None] * np.cos(phase), window[:, None] * np.sin(phase)], axis=1)
    return table.astype(ml_dtypes.bfloat16)


def pair_table():
    columns = build_table().T
    even = np.pad(columns, ((0, 0), (0, SEGLEN)))
    odd = np.pad(columns, ((0, 0), (HALF, HALF)))
    return np.concatenate([even, odd], axis=0)


def split3(value):
    high = value.astype(jnp.bfloat16)
    rest = value - high.astype(jnp.float32)
    middle = rest.astype(jnp.bfloat16)
    low = (rest - middle.astype(jnp.float32)).astype(jnp.bfloat16)
    return high, middle, low


def moments_kernel(
    blocks, channels, tiles, damages, labels, strain, table, influence, out, xs, even, odd, weights, parts
):
    block = pl.program_id(0)
    hotspots = influence.shape[1]
    freq_count = SEGLEN // 2

    @pl.when(block == 0)
    def _():
        xs[tiles * STRIDE :, :] = jnp.zeros((xs.shape[0] - tiles * STRIDE, LANES), jnp.float32)
        weights[...] = jnp.zeros_like(weights)
        for part in range(3):
            weights[part * CPAD : part * CPAD + channels, :] = influence[...]

    for tile in range(tiles):
        xs[tile * STRIDE : tile * STRIDE + channels, :] = strain[
            0, :, tile * LANES : (tile + 1) * LANES
        ].astype(jnp.float32)

    pair_rows = table[...]
    spare = jnp.zeros((LANES - WINDOWS, 2 * LANES), jnp.bfloat16)
    for pair in range(channels // 2):
        windows = []
        for channel in (2 * pair, 2 * pair + 1):
            here = xs[pl.ds(channel, WINDOWS, stride=STRIDE), :].astype(jnp.bfloat16)
            after = xs[pl.ds(channel + STRIDE, WINDOWS, stride=STRIDE), :].astype(jnp.bfloat16)
            windows += [jnp.concatenate([here, after], axis=1), spare]
        window = jnp.concatenate(windows, axis=0)
        coeffs = lax.dot_general(pair_rows, window, NT, preferred_element_type=jnp.float32)
        for offset in range(2):
            channel = 2 * pair + offset
            lanes = slice(offset * LANES, (offset + 1) * LANES)
            even[pl.ds(channel, SEGLEN, stride=STRIDE), :] = coeffs[:SEGLEN, lanes]
            odd[pl.ds(channel, SEGLEN, stride=STRIDE), :] = coeffs[SEGLEN:, lanes]

    lane = lax.broadcasted_iota(jnp.int32, (1, LANES), 1)
    keep_odd = lane < tiles - 1
    first_half = lane[:, : 2 * channels] < channels
    half_index = jnp.where(first_half, 1, 2).astype(jnp.float32)
    scale = 8.0 / (3.0 * SEGLEN * NSEG)

    totals = [jnp.zeros((channels, 2 * channels), jnp.float32)] * NMOM
    for pair in range(freq_count // 2):
        sides = []
        for freq in (2 * pair, 2 * pair + 1):
            pieces = []
            for line in (freq, freq + freq_count):
                rows = slice(line * STRIDE, line * STRIDE + channels)
                pieces.append(even[rows, :].astype(jnp.bfloat16))
                pieces.append(jnp.where(keep_odd, odd[rows, :].astype(jnp.bfloat16), jnp.bfloat16(0)))
            sides.append(jnp.concatenate(pieces, axis=1))
        both = jnp.concatenate(sides, axis=0)
        product = lax.dot_general(both, both, NT, preferred_element_type=jnp.float32)
        cospec = jnp.where(first_half, product[:channels], product[channels:]) * scale
        cospec = cospec.astype(jnp.bfloat16).astype(jnp.float32)
        frequency = (half_index + 2.0 * pair) * (1.0 / SEGLEN)
        square = frequency * frequency
        totals[0] = totals[0] + cospec
        totals[1] = totals[1] + cospec * frequency
        totals[2] = totals[2] + cospec * square
        totals[3] = totals[3] + cospec * (square * square)

    for moment in range(NMOM):
        whole = (totals[moment][:, :channels] + totals[moment][:, channels:]) * (1.0 / SEGLEN)
        whole = jnp.concatenate([whole, jnp.zeros((channels, CPAD - channels), jnp.float32)] * 2, axis=1)
        high, middle, low = split3(whole)
        start = pl.multiple_of((moment * blocks + block) * channels, 16)
        parts[pl.ds(start, channels), :LANES] = jnp.where(lane < CPAD, high, middle)
        parts[pl.ds(start, channels), LANES:] = low

    @pl.when(block == blocks - 1)
    def _():
        width = 2 * LANES
        for step in range(hotspots // width):
            lanes = slice(step * width, (step + 1) * width)
            column = influence[:, lanes].astype(jnp.float32)
            values = []
            for moment in range(NMOM):
                rows = slice(moment * blocks * channels, (moment + 1) * blocks * channels)
                spread = jnp.dot(parts[rows, :], weights[:, lanes], preferred_element_type=jnp.float32)
                spread = spread.reshape(blocks, channels, width)
                values.append(jnp.sum(spread * column[None], axis=1))
            if damages:
                values = [dirlik(*values)]
            for half in range(2):
                start = (2 * step + half) * out.shape[0] // (hotspots // LANES)
                for value in values:
                    out[start : start + blocks, :] = value[:, half * LANES : (half + 1) * LANES]
                    start += blocks
        lanes = lax.broadcasted_iota(jnp.int32, (1, LANES), 1)
        named = jnp.zeros((1, LANES), jnp.float32)
        for index in range(blocks):
            label = (labels[0, index] * NDIR + labels[1, index]) * NYAW + labels[2, index]
            named = jnp.where(lanes % blocks == index, label.astype(jnp.float32), named)
        part = out.shape[0] // (hotspots // LANES)
        for step in range(hotspots // LANES):
            out[(step + 1) * part - 1 : (step + 1) * part, :] = named


def local_rows(strain, bin_labels, influence, damages):
    blocks, channels, samples = strain.shape
    hotspots = influence.shape[0]
    tiles = samples // LANES
    rows = ((1 if damages else NMOM) * blocks + 1) * (hotspots // LANES)
    return pl.pallas_call(
        functools.partial(moments_kernel, blocks, channels, tiles, damages),
        grid=(blocks,),
        in_specs=[
            pl.BlockSpec(memory_space=pltpu.SMEM),
            pl.BlockSpec((1, channels, samples), lambda b: (b, 0, 0)),
            pl.BlockSpec((2 * SEGLEN, 2 * SEGLEN), lambda b: (0, 0)),
            pl.BlockSpec((channels, hotspots), lambda b: (0, 0)),
        ],
        out_specs=pl.BlockSpec((rows, LANES), lambda b: (0, 0)),
        out_shape=jax.ShapeDtypeStruct((rows, LANES), jnp.float32),
        scratch_shapes=[
            pltpu.VMEM(((WINDOWS + 1) * STRIDE, LANES), jnp.float32),
            pltpu.VMEM((SEGLEN * STRIDE, LANES), jnp.float32),
            pltpu.VMEM((SEGLEN * STRIDE, LANES), jnp.float32),
            pltpu.VMEM((2 * LANES, hotspots), jnp.bfloat16),
            pltpu.VMEM((NMOM * blocks * channels, 2 * LANES), jnp.bfloat16),
        ],
        compiler_params=pltpu.CompilerParams(vmem_limit_bytes=60 << 20),
        name="block_moments",
    )(bin_labels.T, strain, jnp.asarray(pair_table()), influence.T)


def dirlik(moment_zero, moment_one, moment_two, moment_four):
    spread_ratio = moment_two / jnp.sqrt(moment_zero * moment_four)
    mean_freq = moment_one / moment_zero * jnp.sqrt(moment_two / moment_four)
    d_one = 2.0 * (mean_freq - spread_ratio**2) / (1.0 + spread_ratio**2)
    shared = 1.0 - spread_ratio - d_one + d_one**2
    r_ratio = (spread_ratio - mean_freq - d_one**2) / shared
    d_two = shared / (1.0 - r_ratio)
    d_three = 1.0 - d_one - d_two
    q_factor = 1.25 * (spread_ratio - d_three - d_two * r_ratio) / d_one
    peak_rate = jnp.sqrt(moment_four / moment_two)
    bracket = 6.0 * d_one * q_factor**3 + 2.8284271247 * 1.3293403882 * (
        jnp.abs(r_ratio) ** 3 * d_two + d_three
    )
    return peak_rate * (2.0 * jnp.sqrt(moment_zero)) ** 3 * bracket


def gather_kernel(sources, received, damage, total):
    count_blocks, width = damage.shape
    blocks = count_blocks // sources
    part = blocks + 1
    by_block = jnp.concatenate(
        [received[source * part : source * part + blocks, :] for source in range(sources)], axis=0
    )
    named = jnp.concatenate(
        [received[(source + 1) * part - 1 : (source + 1) * part, :] for source in range(sources)], axis=0
    )
    source = lax.broadcasted_iota(jnp.int32, named.shape, 0)
    lane = lax.broadcasted_iota(jnp.int32, named.shape, 1)
    named = jnp.sum(jnp.where(lane // blocks == source, named, 0.0), axis=0, keepdims=True)
    bins = lax.broadcasted_iota(jnp.int32, (NBIN, count_blocks), 0).astype(jnp.float32)
    chosen = jnp.where(named == bins, 1.0, 0.0).astype(jnp.bfloat16)
    by_bin = jnp.zeros((NBIN, width), jnp.float32)
    for piece in split3(by_block):
        by_bin = by_bin + jnp.dot(chosen, piece, preferred_element_type=jnp.float32)
    damage[...] = by_bin
    total[...] = jnp.sum(by_block * (1.0 / count_blocks), axis=0, keepdims=True)


def bin_kernel(named, moments, damage, total):
    count_blocks = named.shape[1]
    bins = lax.broadcasted_iota(jnp.int32, (NBIN, count_blocks), 0).astype(jnp.float32)
    member = jnp.where(named[...] == bins, 1.0, 0.0)
    count = jnp.sum(member, axis=1, keepdims=True)
    chosen = member.astype(jnp.bfloat16)
    means = []
    for moment in range(NMOM):
        total_moment = jnp.zeros(damage.shape, jnp.float32)
        for piece in split3(moments[moment]):
            total_moment = total_moment + jnp.dot(chosen, piece, preferred_element_type=jnp.float32)
        means.append(total_moment / count)
    by_bin = dirlik(*means)
    damage[...] = by_bin
    total[...] = jnp.sum(count / count_blocks * by_bin, axis=0, keepdims=True)


def per_device(strain, bin_labels, influence):
    devices = lax.axis_size("tm")
    blocks = strain.shape[0]
    hotspots = influence.shape[0]
    width = hotspots // devices
    out_shape = (
        jax.ShapeDtypeStruct((NBIN, width), jnp.float32),
        jax.ShapeDtypeStruct((1, width), jnp.float32),
    )
    if blocks * devices == NBIN and width == LANES:
        rows = local_rows(strain, bin_labels, influence, True)
        rows = rows.reshape(devices, 1, (blocks + 1) * LANES)
        received = lax.all_to_all(rows, "tm", split_axis=0, concat_axis=0, tiled=True)
        damage, total = pl.pallas_call(
            functools.partial(gather_kernel, devices), out_shape=out_shape, name="gather_damage"
        )(received.reshape(devices * (blocks + 1), LANES))
        return damage, total.reshape(width)
    rows = local_rows(strain, bin_labels, influence, False)
    rows = rows.reshape(hotspots // LANES, NMOM * blocks + 1, LANES)
    named = jnp.broadcast_to(rows[:1, -1, :blocks], (devices, blocks))
    moments = rows[:, :-1].reshape(hotspots // LANES, NMOM, blocks, LANES)
    moments = moments.transpose(1, 2, 0, 3).reshape(NMOM, blocks, devices, width)
    moments = moments.transpose(2, 0, 1, 3).reshape(devices, NMOM * blocks * width)
    sent = jnp.concatenate([moments, named], axis=1)
    received = lax.all_to_all(sent, "tm", split_axis=0, concat_axis=0, tiled=True)
    named = received[:, -blocks:].reshape(1, devices * blocks)
    moments = received[:, :-blocks].reshape(devices, NMOM, blocks, width)
    moments = moments.transpose(1, 0, 2, 3).reshape(NMOM, devices * blocks, width)
    damage, total = pl.pallas_call(bin_kernel, out_shape=out_shape, name="bin_damage")(named, moments)
    return damage, total.reshape(width)


def solution(mesh):
    placed = (P(("groups", "tm"), None, None), P(("groups", "tm"), None), P())
    return jax.shard_map(
        per_device,
        mesh=mesh,
        in_specs=placed,
        out_specs=(P("groups", "tm"), P(("groups", "tm"))),
        check_vma=False,
    )
```

```python
import functools
import math

import jax
import jax.numpy as jnp
import ml_dtypes
import numpy as np
from jax import lax
from jax.experimental import pallas as pl
from jax.experimental.pallas import tpu as pltpu
from jax.sharding import PartitionSpec as P

SEGLEN = 128
NSEG = 187
NDIR = 8
NYAW = 2
NBIN = 128
LANES = 128
HALF = SEGLEN // 2
CPAD = 64
NMOM = 4
WINDOWS = 96
STRIDE = 49
XSHARE = 0
GROUP = 2
NT = (((1,), (1,)), ((), ()))


def build_table():
    positions = np.arange(SEGLEN)
    harmonic = np.arange(1, SEGLEN // 2 + 1)
    phase = (positions[:, None] * harmonic[None, :] % SEGLEN) * (2.0 * math.pi / SEGLEN)
    window = 0.5 - 0.5 * np.cos(positions * (2.0 * math.pi / SEGLEN))
    table = np.concatenate([window[:, None] * np.cos(phase), window[:, None] * np.sin(phase)], axis=1)
    return table.astype(ml_dtypes.bfloat16)


def pair_table():
    columns = build_table().T
    even = np.pad(columns, ((0, 0), (0, SEGLEN)))
    odd = np.pad(columns, ((0, 0), (HALF, HALF)))
    return np.concatenate([even, odd], axis=0)


def split3(value):
    high = value.astype(jnp.bfloat16)
    rest = value - high.astype(jnp.float32)
    middle = rest.astype(jnp.bfloat16)
    low = (rest - middle.astype(jnp.float32)).astype(jnp.bfloat16)
    return high, middle, low


def spread_samples(strain, xs, tile):
    channels = strain.shape[1]
    xs[tile * STRIDE : tile * STRIDE + channels, :] = strain[
        0, :, tile * LANES : (tile + 1) * LANES
    ].astype(jnp.float32)


def transform(table, xs, even, odd, pair):
    spare = jnp.zeros((LANES - WINDOWS, 2 * LANES), jnp.bfloat16)
    windows = []
    for channel in (2 * pair, 2 * pair + 1):
        here = xs[pl.ds(channel, WINDOWS, stride=STRIDE), :].astype(jnp.bfloat16)
        after = xs[pl.ds(channel + STRIDE, WINDOWS, stride=STRIDE), :].astype(jnp.bfloat16)
        windows += [jnp.concatenate([here, after], axis=1), spare]
    window = jnp.concatenate(windows, axis=0)
    coeffs = lax.dot_general(table[...], window, NT, preferred_element_type=jnp.float32)
    for offset in range(2):
        channel = 2 * pair + offset
        lanes = slice(offset * LANES, (offset + 1) * LANES)
        even[pl.ds(channel, SEGLEN, stride=STRIDE), :] = coeffs[:SEGLEN, lanes]
        odd[pl.ds(channel, SEGLEN, stride=STRIDE), :] = coeffs[SEGLEN:, lanes]


def add_cross(channels, keep_odd, even, odd, pair, totals):
    freq_count = SEGLEN // 2
    sides = []
    for freq in (2 * pair, 2 * pair + 1):
        pieces = []
        for line in (freq, freq + freq_count):
            rows = slice(line * STRIDE, line * STRIDE + channels)
            pieces.append(even[rows, :].astype(jnp.bfloat16))
            pieces.append(jnp.where(keep_odd, odd[rows, :].astype(jnp.bfloat16), jnp.bfloat16(0)))
        sides.append(jnp.concatenate(pieces, axis=1))
    both = jnp.concatenate(sides, axis=0)
    product = lax.dot_general(both, both, NT, preferred_element_type=jnp.float32)
    first_half = lax.broadcasted_iota(jnp.int32, (1, 2 * channels), 1) < channels
    scale = 8.0 / (3.0 * SEGLEN * NSEG)
    cospec = jnp.where(first_half, product[:channels], product[channels:]) * scale
    cospec = cospec.astype(jnp.bfloat16).astype(jnp.float32)
    frequency = jnp.where(first_half, (2 * pair + 1) / SEGLEN, (2 * pair + 2) / SEGLEN)
    square = frequency * frequency
    totals[0] = totals[0] + cospec
    totals[1] = totals[1] + cospec * frequency
    totals[2] = totals[2] + cospec * square
    totals[3] = totals[3] + cospec * (square * square)


def moments_kernel(
    blocks, channels, tiles, damages, labels, strain, table, influence, out, xs, even0, odd0, even1, odd1, weights, parts
):
    step_index = pl.program_id(0)
    hotspots = influence.shape[1]
    pairs = channels // 2
    lines = SEGLEN // 4
    slots = ((even0, odd0), (even1, odd1))
    lane = lax.broadcasted_iota(jnp.int32, (1, LANES), 1)
    keep_odd = lane < tiles - 1

    def work(source, target):
        totals = [jnp.zeros((channels, 2 * channels), jnp.float32)] * NMOM
        done = 0

        def catch_up(goal):
            nonlocal done
            while source is not None and done < min(goal, lines):
                add_cross(channels, keep_odd, *slots[source], done, totals)
                done += 1

        if target is not None:
            for tile in range(tiles):
                spread_samples(strain, xs, tile)
                catch_up((tile + 1) * XSHARE // tiles)
            for pair in range(pairs):
                transform(table, xs, *slots[target], pair)
                catch_up(XSHARE + (pair + 1) * (lines - XSHARE) // pairs)
        catch_up(lines)
        if source is None:
            return
        block = step_index - 1
        for moment in range(NMOM):
            whole = (totals[moment][:, :channels] + totals[moment][:, channels:]) * (1.0 / SEGLEN)
            gap = jnp.zeros((channels, CPAD - channels), jnp.float32)
            high, middle, low = split3(jnp.concatenate([whole, gap] * 2, axis=1))
            start = pl.multiple_of((moment * blocks + block) * channels, 16)
            parts[pl.ds(start, channels), :LANES] = jnp.where(lane < CPAD, high, middle)
            parts[pl.ds(start, channels), LANES:] = low

    @pl.when(step_index == 0)
    def _():
        xs[tiles * STRIDE :, :] = jnp.zeros((xs.shape[0] - tiles * STRIDE, LANES), jnp.float32)
        weights[...] = jnp.zeros_like(weights)
        for part in range(3):
            weights[part * CPAD : part * CPAD + channels, :] = influence[...]
        work(None, 0)

    for parity in range(2):

        @pl.when((step_index > 0) & (step_index < blocks) & (step_index % 2 == parity))
        def _():
            work(1 - parity, parity)

    @pl.when(step_index == blocks)
    def _():
        work((blocks - 1) % 2, None)
        width = 2 * LANES
        count = hotspots // width
        part = out.shape[0] // (hotspots // LANES)
        for first in range(0, count, GROUP):
            values = []
            for moment in range(NMOM):
                rows = slice(moment * blocks * channels, (moment + 1) * blocks * channels)
                values.append([])
                for step in range(first, first + GROUP):
                    lanes = slice(step * width, (step + 1) * width)
                    column = influence[:, lanes].astype(jnp.float32)
                    spread = jnp.dot(parts[rows, :], weights[:, lanes], preferred_element_type=jnp.float32)
                    spread = spread.reshape(blocks, channels, width)
                    values[-1].append(jnp.sum(spread * column[None], axis=1))
            values = [jnp.concatenate(value, axis=1) for value in values]
            if damages:
                values = [dirlik(*values)]
            for half in range(2 * GROUP):
                start = (2 * first + half) * part
                for value in values:
                    out[start : start + blocks, :] = value[:, half * LANES : (half + 1) * LANES]
                    start += blocks
        named = jnp.zeros((1, LANES), jnp.float32)
        for index in range(blocks):
            label = (labels[0, index] * NDIR + labels[1, index]) * NYAW + labels[2, index]
            named = jnp.where(lane % blocks == index, label.astype(jnp.float32), named)
        for step in range(hotspots // LANES):
            out[(step + 1) * part - 1 : (step + 1) * part, :] = named


def local_rows(strain, bin_labels, influence, damages):
    blocks, channels, samples = strain.shape
    hotspots = influence.shape[0]
    tiles = samples // LANES
    rows = ((1 if damages else NMOM) * blocks + 1) * (hotspots // LANES)
    return pl.pallas_call(
        functools.partial(moments_kernel, blocks, channels, tiles, damages),
        grid=(blocks + 1,),
        in_specs=[
            pl.BlockSpec(memory_space=pltpu.SMEM),
            pl.BlockSpec((1, channels, samples), lambda b: (jnp.minimum(b, blocks - 1), 0, 0)),
            pl.BlockSpec((2 * SEGLEN, 2 * SEGLEN), lambda b: (0, 0)),
            pl.BlockSpec((channels, hotspots), lambda b: (0, 0)),
        ],
        out_specs=pl.BlockSpec((rows, LANES), lambda b: (0, 0)),
        out_shape=jax.ShapeDtypeStruct((rows, LANES), jnp.float32),
        scratch_shapes=[
            pltpu.VMEM(((WINDOWS + 1) * STRIDE, LANES), jnp.float32),
            *[pltpu.VMEM((SEGLEN * STRIDE, LANES), jnp.float32)] * 4,
            pltpu.VMEM((2 * LANES, hotspots), jnp.bfloat16),
            pltpu.VMEM((NMOM * blocks * channels, 2 * LANES), jnp.bfloat16),
        ],
        compiler_params=pltpu.CompilerParams(vmem_limit_bytes=60 << 20),
        name="block_moments",
    )(bin_labels.T, strain, jnp.asarray(pair_table()), influence.T)


def dirlik(moment_zero, moment_one, moment_two, moment_four):
    spread_ratio = moment_two / jnp.sqrt(moment_zero * moment_four)
    mean_freq = moment_one / moment_zero * jnp.sqrt(moment_two / moment_four)
    d_one = 2.0 * (mean_freq - spread_ratio**2) / (1.0 + spread_ratio**2)
    shared = 1.0 - spread_ratio - d_one + d_one**2
    r_ratio = (spread_ratio - mean_freq - d_one**2) / shared
    d_two = shared / (1.0 - r_ratio)
    d_three = 1.0 - d_one - d_two
    q_factor = 1.25 * (spread_ratio - d_three - d_two * r_ratio) / d_one
    peak_rate = jnp.sqrt(moment_four / moment_two)
    bracket = 6.0 * d_one * q_factor**3 + 2.8284271247 * 1.3293403882 * (
        jnp.abs(r_ratio) ** 3 * d_two + d_three
    )
    return peak_rate * (2.0 * jnp.sqrt(moment_zero)) ** 3 * bracket


def gather_kernel(sources, received, damage, total):
    count_blocks, width = damage.shape
    blocks = count_blocks // sources
    part = blocks + 1
    by_block = jnp.concatenate(
        [received[source * part : source * part + blocks, :] for source in range(sources)], axis=0
    )
    named = jnp.concatenate(
        [received[(source + 1) * part - 1 : (source + 1) * part, :] for source in range(sources)], axis=0
    )
    source = lax.broadcasted_iota(jnp.int32, named.shape, 0)
    lane = lax.broadcasted_iota(jnp.int32, named.shape, 1)
    named = jnp.sum(jnp.where(lane // blocks == source, named, 0.0), axis=0, keepdims=True)
    bins = lax.broadcasted_iota(jnp.int32, (NBIN, count_blocks), 0).astype(jnp.float32)
    chosen = jnp.where(named == bins, 1.0, 0.0).astype(jnp.bfloat16)
    by_bin = jnp.zeros((NBIN, width), jnp.float32)
    for piece in split3(by_block):
        by_bin = by_bin + jnp.dot(chosen, piece, preferred_element_type=jnp.float32)
    damage[...] = by_bin
    total[...] = jnp.sum(by_block * (1.0 / count_blocks), axis=0, keepdims=True)


def bin_kernel(named, moments, damage, total):
    count_blocks = named.shape[1]
    bins = lax.broadcasted_iota(jnp.int32, (NBIN, count_blocks), 0).astype(jnp.float32)
    member = jnp.where(named[...] == bins, 1.0, 0.0)
    count = jnp.sum(member, axis=1, keepdims=True)
    chosen = member.astype(jnp.bfloat16)
    means = []
    for moment in range(NMOM):
        total_moment = jnp.zeros(damage.shape, jnp.float32)
        for piece in split3(moments[moment]):
            total_moment = total_moment + jnp.dot(chosen, piece, preferred_element_type=jnp.float32)
        means.append(total_moment / count)
    by_bin = dirlik(*means)
    damage[...] = by_bin
    total[...] = jnp.sum(count / count_blocks * by_bin, axis=0, keepdims=True)


def per_device(strain, bin_labels, influence):
    devices = lax.axis_size("tm")
    blocks = strain.shape[0]
    hotspots = influence.shape[0]
    width = hotspots // devices
    out_shape = (
        jax.ShapeDtypeStruct((NBIN, width), jnp.float32),
        jax.ShapeDtypeStruct((1, width), jnp.float32),
    )
    if blocks * devices == NBIN and width == LANES:
        rows = local_rows(strain, bin_labels, influence, True)
        rows = rows.reshape(devices, 1, (blocks + 1) * LANES)
        received = lax.all_to_all(rows, "tm", split_axis=0, concat_axis=0, tiled=True)
        damage, total = pl.pallas_call(
            functools.partial(gather_kernel, devices), out_shape=out_shape, name="gather_damage"
        )(received.reshape(devices * (blocks + 1), LANES))
        return damage, total.reshape(width)
    rows = local_rows(strain, bin_labels, influence, False)
    rows = rows.reshape(hotspots // LANES, NMOM * blocks + 1, LANES)
    named = jnp.broadcast_to(rows[:1, -1, :blocks], (devices, blocks))
    moments = rows[:, :-1].reshape(hotspots // LANES, NMOM, blocks, LANES)
    moments = moments.transpose(1, 2, 0, 3).reshape(NMOM, blocks, devices, width)
    moments = moments.transpose(2, 0, 1, 3).reshape(devices, NMOM * blocks * width)
    sent = jnp.concatenate([moments, named], axis=1)
    received = lax.all_to_all(sent, "tm", split_axis=0, concat_axis=0, tiled=True)
    named = received[:, -blocks:].reshape(1, devices * blocks)
    moments = received[:, :-blocks].reshape(devices, NMOM, blocks, width)
    moments = moments.transpose(1, 0, 2, 3).reshape(NMOM, devices * blocks, width)
    damage, total = pl.pallas_call(bin_kernel, out_shape=out_shape, name="bin_damage")(named, moments)
    return damage, total.reshape(width)


def solution(mesh):
    placed = (P(("groups", "tm"), None, None), P(("groups", "tm"), None), P())
    return jax.shard_map(
        per_device,
        mesh=mesh,
        in_specs=placed,
        out_specs=(P("groups", "tm"), P(("groups", "tm"))),
        check_vma=False,
    )
```

```python
import functools
import math

import jax
import jax.numpy as jnp
import ml_dtypes
import numpy as np
from jax import lax
from jax.experimental import pallas as pl
from jax.experimental.pallas import tpu as pltpu
from jax.sharding import PartitionSpec as P

SEGLEN = 128
NSEG = 187
NDIR = 8
NYAW = 2
NBIN = 128
LANES = 128
HALF = SEGLEN // 2
CPAD = 64
NMOM = 4
WINDOWS = 96
STRIDE = 49
GROUP = 2
NT = (((1,), (1,)), ((), ()))


def build_table():
    positions = np.arange(SEGLEN)
    harmonic = np.arange(1, SEGLEN // 2 + 1)
    phase = (positions[:, None] * harmonic[None, :] % SEGLEN) * (2.0 * math.pi / SEGLEN)
    window = 0.5 - 0.5 * np.cos(positions * (2.0 * math.pi / SEGLEN))
    table = np.concatenate([window[:, None] * np.cos(phase), window[:, None] * np.sin(phase)], axis=1)
    return table.astype(ml_dtypes.bfloat16)


def pair_table():
    columns = build_table().T
    even = np.pad(columns, ((0, 0), (0, SEGLEN)))
    odd = np.pad(columns, ((0, 0), (HALF, HALF)))
    return np.concatenate([even, odd], axis=0)


def split3(value):
    high = value.astype(jnp.bfloat16)
    rest = value - high.astype(jnp.float32)
    middle = rest.astype(jnp.bfloat16)
    low = (rest - middle.astype(jnp.float32)).astype(jnp.bfloat16)
    return high, middle, low


def spread_samples(strain, xs, tile):
    channels = strain.shape[1]
    xs[tile * STRIDE : tile * STRIDE + channels, :] = strain[
        0, :, tile * LANES : (tile + 1) * LANES
    ].astype(jnp.float32)


def transform(table, xs, even, odd, pair):
    spare = jnp.zeros((LANES - WINDOWS, 2 * LANES), jnp.bfloat16)
    windows = []
    for channel in (2 * pair, 2 * pair + 1):
        here = xs[pl.ds(channel, WINDOWS, stride=STRIDE), :].astype(jnp.bfloat16)
        after = xs[pl.ds(channel + STRIDE, WINDOWS, stride=STRIDE), :].astype(jnp.bfloat16)
        windows += [jnp.concatenate([here, after], axis=1), spare]
    window = jnp.concatenate(windows, axis=0)
    coeffs = lax.dot_general(table[...], window, NT, preferred_element_type=jnp.float32)
    for offset in range(2):
        channel = 2 * pair + offset
        lanes = slice(offset * LANES, (offset + 1) * LANES)
        even[pl.ds(channel, SEGLEN, stride=STRIDE), :] = coeffs[:SEGLEN, lanes]
        odd[pl.ds(channel, SEGLEN, stride=STRIDE), :] = coeffs[SEGLEN:, lanes]


def add_cross(channels, keep_odd, even, odd, pair, totals):
    freq_count = SEGLEN // 2
    sides = []
    for freq in (2 * pair, 2 * pair + 1):
        pieces = []
        for line in (freq, freq + freq_count):
            rows = slice(line * STRIDE, line * STRIDE + channels)
            pieces.append(even[rows, :].astype(jnp.bfloat16))
            pieces.append(jnp.where(keep_odd, odd[rows, :].astype(jnp.bfloat16), jnp.bfloat16(0)))
        sides.append(jnp.concatenate(pieces, axis=1))
    both = jnp.concatenate(sides, axis=0)
    product = lax.dot_general(both, both, NT, preferred_element_type=jnp.float32)
    first_half = lax.broadcasted_iota(jnp.int32, (1, 2 * channels), 1) < channels
    scale = 8.0 / (3.0 * SEGLEN * NSEG)
    cospec = jnp.where(first_half, product[:channels], product[channels:]) * scale
    cospec = cospec.astype(jnp.bfloat16).astype(jnp.float32)
    frequency = jnp.where(first_half, (2 * pair + 1) / SEGLEN, (2 * pair + 2) / SEGLEN)
    square = frequency * frequency
    totals[0] = totals[0] + cospec
    totals[1] = totals[1] + cospec * frequency
    totals[2] = totals[2] + cospec * square
    totals[3] = totals[3] + cospec * (square * square)


def moments_kernel(
    blocks, channels, tiles, damages, labels, strain, table, influence, out, xs, even0, odd0, even1, odd1, weights, parts
):
    step_index = pl.program_id(0)
    hotspots = influence.shape[1]
    pairs = channels // 2
    lines = SEGLEN // 4
    slots = ((even0, odd0), (even1, odd1))
    lane = lax.broadcasted_iota(jnp.int32, (1, LANES), 1)
    keep_odd = lane < tiles - 1

    def work(source, target, index=0):
        totals = [jnp.zeros((channels, 2 * channels), jnp.float32)] * NMOM
        done = 0

        def catch_up(goal):
            nonlocal done
            while source is not None and done < min(goal, lines):
                add_cross(channels, keep_odd, *slots[source], done, totals)
                done += 1

        if target is not None:
            for tile in range(tiles):
                spread_samples(strain.at[index : index + 1], xs, tile)
            for pair in range(pairs):
                transform(table, xs, *slots[target], pair)
                catch_up((pair + 1) * lines // pairs)
        catch_up(lines)
        if source is None:
            return
        block = 2 * step_index + index - 1
        for moment in range(NMOM):
            whole = (totals[moment][:, :channels] + totals[moment][:, channels:]) * (1.0 / SEGLEN)
            gap = jnp.zeros((channels, CPAD - channels), jnp.float32)
            high, middle, low = split3(jnp.concatenate([whole, gap] * 2, axis=1))
            start = pl.multiple_of((moment * blocks + block) * channels, 16)
            parts[pl.ds(start, channels), :LANES] = jnp.where(lane < CPAD, high, middle)
            parts[pl.ds(start, channels), LANES:] = low

    @pl.when(step_index == 0)
    def _():
        xs[tiles * STRIDE :, :] = jnp.zeros((xs.shape[0] - tiles * STRIDE, LANES), jnp.float32)
        weights[...] = jnp.zeros_like(weights)
        for part in range(3):
            weights[part * CPAD : part * CPAD + channels, :] = influence[...]
        work(None, 0, 0)
        work(0, 1, 1)

    @pl.when((step_index > 0) & (step_index < blocks // 2))
    def _():
        work(1, 0, 0)
        work(0, 1, 1)

    @pl.when(step_index == blocks // 2)
    def _():
        work(1, None, 0)
        width = 2 * LANES
        count = hotspots // width
        part = out.shape[0] // (hotspots // LANES)
        for first in range(0, count, GROUP):
            values = []
            for moment in range(NMOM):
                rows = slice(moment * blocks * channels, (moment + 1) * blocks * channels)
                values.append([])
                for step in range(first, first + GROUP):
                    lanes = slice(step * width, (step + 1) * width)
                    column = influence[:, lanes].astype(jnp.float32)
                    spread = jnp.dot(parts[rows, :], weights[:, lanes], preferred_element_type=jnp.float32)
                    spread = spread.reshape(blocks, channels, width)
                    values[-1].append(jnp.sum(spread * column[None], axis=1))
            values = [jnp.concatenate(value, axis=1) for value in values]
            if damages:
                values = [dirlik(*values)]
            for half in range(2 * GROUP):
                start = (2 * first + half) * part
                for value in values:
                    out[start : start + blocks, :] = value[:, half * LANES : (half + 1) * LANES]
                    start += blocks
        named = jnp.zeros((1, LANES), jnp.float32)
        for index in range(blocks):
            label = (labels[0, index] * NDIR + labels[1, index]) * NYAW + labels[2, index]
            named = jnp.where(lane % blocks == index, label.astype(jnp.float32), named)
        for step in range(hotspots // LANES):
            out[(step + 1) * part - 1 : (step + 1) * part, :] = named


def local_rows(strain, bin_labels, influence, damages):
    blocks, channels, samples = strain.shape
    hotspots = influence.shape[0]
    tiles = samples // LANES
    rows = ((1 if damages else NMOM) * blocks + 1) * (hotspots // LANES)
    return pl.pallas_call(
        functools.partial(moments_kernel, blocks, channels, tiles, damages),
        grid=(blocks // 2 + 1,),
        in_specs=[
            pl.BlockSpec(memory_space=pltpu.SMEM),
            pl.BlockSpec((2, channels, samples), lambda b: (jnp.minimum(b, blocks // 2 - 1), 0, 0)),
            pl.BlockSpec((2 * SEGLEN, 2 * SEGLEN), lambda b: (0, 0)),
            pl.BlockSpec((channels, hotspots), lambda b: (0, 0)),
        ],
        out_specs=pl.BlockSpec((rows, LANES), lambda b: (0, 0)),
        out_shape=jax.ShapeDtypeStruct((rows, LANES), jnp.float32),
        scratch_shapes=[
            pltpu.VMEM(((WINDOWS + 1) * STRIDE, LANES), jnp.float32),
            *[pltpu.VMEM((SEGLEN * STRIDE, LANES), jnp.float32)] * 4,
            pltpu.VMEM((2 * LANES, hotspots), jnp.bfloat16),
            pltpu.VMEM((NMOM * blocks * channels, 2 * LANES), jnp.bfloat16),
        ],
        compiler_params=pltpu.CompilerParams(vmem_limit_bytes=60 << 20),
        name="block_moments",
    )(bin_labels.T, strain, jnp.asarray(pair_table()), influence.T)


def dirlik(moment_zero, moment_one, moment_two, moment_four):
    spread_ratio = moment_two / jnp.sqrt(moment_zero * moment_four)
    mean_freq = moment_one / moment_zero * jnp.sqrt(moment_two / moment_four)
    d_one = 2.0 * (mean_freq - spread_ratio**2) / (1.0 + spread_ratio**2)
    shared = 1.0 - spread_ratio - d_one + d_one**2
    r_ratio = (spread_ratio - mean_freq - d_one**2) / shared
    d_two = shared / (1.0 - r_ratio)
    d_three = 1.0 - d_one - d_two
    q_factor = 1.25 * (spread_ratio - d_three - d_two * r_ratio) / d_one
    peak_rate = jnp.sqrt(moment_four / moment_two)
    bracket = 6.0 * d_one * q_factor**3 + 2.8284271247 * 1.3293403882 * (
        jnp.abs(r_ratio) ** 3 * d_two + d_three
    )
    return peak_rate * (2.0 * jnp.sqrt(moment_zero)) ** 3 * bracket


def gather_kernel(sources, received, damage, total):
    count_blocks, width = damage.shape
    blocks = count_blocks // sources
    part = blocks + 1
    by_block = jnp.concatenate(
        [received[source * part : source * part + blocks, :] for source in range(sources)], axis=0
    )
    named = jnp.concatenate(
        [received[(source + 1) * part - 1 : (source + 1) * part, :] for source in range(sources)], axis=0
    )
    source = lax.broadcasted_iota(jnp.int32, named.shape, 0)
    lane = lax.broadcasted_iota(jnp.int32, named.shape, 1)
    named = jnp.sum(jnp.where(lane // blocks == source, named, 0.0), axis=0, keepdims=True)
    bins = lax.broadcasted_iota(jnp.int32, (NBIN, count_blocks), 0).astype(jnp.float32)
    chosen = jnp.where(named == bins, 1.0, 0.0).astype(jnp.bfloat16)
    by_bin = jnp.zeros((NBIN, width), jnp.float32)
    for piece in split3(by_block):
        by_bin = by_bin + jnp.dot(chosen, piece, preferred_element_type=jnp.float32)
    damage[...] = by_bin
    total[...] = jnp.sum(by_block * (1.0 / count_blocks), axis=0, keepdims=True)


def bin_kernel(named, moments, damage, total):
    count_blocks = named.shape[1]
    bins = lax.broadcasted_iota(jnp.int32, (NBIN, count_blocks), 0).astype(jnp.float32)
    member = jnp.where(named[...] == bins, 1.0, 0.0)
    count = jnp.sum(member, axis=1, keepdims=True)
    chosen = member.astype(jnp.bfloat16)
    means = []
    for moment in range(NMOM):
        total_moment = jnp.zeros(damage.shape, jnp.float32)
        for piece in split3(moments[moment]):
            total_moment = total_moment + jnp.dot(chosen, piece, preferred_element_type=jnp.float32)
        means.append(total_moment / count)
    by_bin = dirlik(*means)
    damage[...] = by_bin
    total[...] = jnp.sum(count / count_blocks * by_bin, axis=0, keepdims=True)


def per_device(strain, bin_labels, influence):
    devices = lax.axis_size("tm")
    blocks = strain.shape[0]
    hotspots = influence.shape[0]
    width = hotspots // devices
    out_shape = (
        jax.ShapeDtypeStruct((NBIN, width), jnp.float32),
        jax.ShapeDtypeStruct((1, width), jnp.float32),
    )
    if blocks * devices == NBIN and width == LANES:
        rows = local_rows(strain, bin_labels, influence, True)
        rows = rows.reshape(devices, 1, (blocks + 1) * LANES)
        received = lax.all_to_all(rows, "tm", split_axis=0, concat_axis=0, tiled=True)
        damage, total = pl.pallas_call(
            functools.partial(gather_kernel, devices), out_shape=out_shape, name="gather_damage"
        )(received.reshape(devices * (blocks + 1), LANES))
        return damage, total.reshape(width)
    rows = local_rows(strain, bin_labels, influence, False)
    rows = rows.reshape(hotspots // LANES, NMOM * blocks + 1, LANES)
    named = jnp.broadcast_to(rows[:1, -1, :blocks], (devices, blocks))
    moments = rows[:, :-1].reshape(hotspots // LANES, NMOM, blocks, LANES)
    moments = moments.transpose(1, 2, 0, 3).reshape(NMOM, blocks, devices, width)
    moments = moments.transpose(2, 0, 1, 3).reshape(devices, NMOM * blocks * width)
    sent = jnp.concatenate([moments, named], axis=1)
    received = lax.all_to_all(sent, "tm", split_axis=0, concat_axis=0, tiled=True)
    named = received[:, -blocks:].reshape(1, devices * blocks)
    moments = received[:, :-blocks].reshape(devices, NMOM, blocks, width)
    moments = moments.transpose(1, 0, 2, 3).reshape(NMOM, devices * blocks, width)
    damage, total = pl.pallas_call(bin_kernel, out_shape=out_shape, name="bin_damage")(named, moments)
    return damage, total.reshape(width)


def solution(mesh):
    placed = (P(("groups", "tm"), None, None), P(("groups", "tm"), None), P())
    return jax.shard_map(
        per_device,
        mesh=mesh,
        in_specs=placed,
        out_specs=(P("groups", "tm"), P(("groups", "tm"))),
        check_vma=False,
    )
```

```python
import functools
import math

import jax
import jax.numpy as jnp
import ml_dtypes
import numpy as np
from jax import lax
from jax.experimental import pallas as pl
from jax.experimental.pallas import tpu as pltpu
from jax.sharding import PartitionSpec as P

SEGLEN = 128
NSEG = 187
NDIR = 8
NYAW = 2
NBIN = 128
LANES = 128
HALF = SEGLEN // 2
CPAD = 64
NMOM = 4
WINDOWS = 96
STRIDE = 49
GROUP = 2
NT = (((1,), (1,)), ((), ()))


def build_table():
    positions = np.arange(SEGLEN)
    harmonic = np.arange(1, SEGLEN // 2 + 1)
    phase = (positions[:, None] * harmonic[None, :] % SEGLEN) * (2.0 * math.pi / SEGLEN)
    window = 0.5 - 0.5 * np.cos(positions * (2.0 * math.pi / SEGLEN))
    table = np.concatenate([window[:, None] * np.cos(phase), window[:, None] * np.sin(phase)], axis=1)
    return table.astype(ml_dtypes.bfloat16)


def pair_table():
    columns = build_table().T
    even = np.pad(columns, ((0, 0), (0, SEGLEN)))
    odd = np.pad(columns, ((0, 0), (HALF, HALF)))
    return np.concatenate([even, odd], axis=0)


def split3(value):
    high = value.astype(jnp.bfloat16)
    rest = value - high.astype(jnp.float32)
    middle = rest.astype(jnp.bfloat16)
    low = (rest - middle.astype(jnp.float32)).astype(jnp.bfloat16)
    return high, middle, low


def spread_samples(strain, xs, tile):
    channels = strain.shape[1]
    xs[tile * STRIDE : tile * STRIDE + channels, :] = strain[
        0, :, tile * LANES : (tile + 1) * LANES
    ].astype(jnp.float32)


def transform(table, xs, even, odd, pair):
    spare = jnp.zeros((LANES - WINDOWS, 2 * LANES), jnp.bfloat16)
    windows = []
    for channel in (2 * pair, 2 * pair + 1):
        here = xs[pl.ds(channel, WINDOWS, stride=STRIDE), :].astype(jnp.bfloat16)
        after = xs[pl.ds(channel + STRIDE, WINDOWS, stride=STRIDE), :].astype(jnp.bfloat16)
        windows += [jnp.concatenate([here, after], axis=1), spare]
    window = jnp.concatenate(windows, axis=0)
    coeffs = lax.dot_general(table[...], window, NT, preferred_element_type=jnp.float32)
    for offset in range(2):
        channel = 2 * pair + offset
        lanes = slice(offset * LANES, (offset + 1) * LANES)
        even[pl.ds(channel, SEGLEN, stride=STRIDE), :] = coeffs[:SEGLEN, lanes]
        odd[pl.ds(channel, SEGLEN, stride=STRIDE), :] = coeffs[SEGLEN:, lanes]


def add_cross(channels, keep_odd, even, odd, pair, totals):
    freq_count = SEGLEN // 2
    sides = []
    for freq in (2 * pair, 2 * pair + 1):
        pieces = []
        for line in (freq, freq + freq_count):
            rows = slice(line * STRIDE, line * STRIDE + channels)
            pieces.append(even[rows, :].astype(jnp.bfloat16))
            pieces.append(jnp.where(keep_odd, odd[rows, :].astype(jnp.bfloat16), jnp.bfloat16(0)))
        sides.append(jnp.concatenate(pieces, axis=1))
    both = jnp.concatenate(sides, axis=0)
    product = lax.dot_general(both, both, NT, preferred_element_type=jnp.float32)
    first_half = lax.broadcasted_iota(jnp.int32, (1, 2 * channels), 1) < channels
    scale = 8.0 / (3.0 * SEGLEN * NSEG)
    cospec = jnp.where(first_half, product[:channels], product[channels:]) * scale
    cospec = cospec.astype(jnp.bfloat16).astype(jnp.float32)
    frequency = jnp.where(first_half, (2 * pair + 1) / SEGLEN, (2 * pair + 2) / SEGLEN)
    square = frequency * frequency
    totals[0] = totals[0] + cospec
    totals[1] = totals[1] + cospec * frequency
    totals[2] = totals[2] + cospec * square
    totals[3] = totals[3] + cospec * (square * square)


def moments_kernel(
    blocks, channels, tiles, damages, labels, strain, table, influence, out, xs, even0, odd0, even1, odd1, weights, parts
):
    step_index = pl.program_id(0)
    hotspots = influence.shape[1]
    pairs = channels // 2
    lines = SEGLEN // 4
    slots = ((even0, odd0), (even1, odd1))
    lane = lax.broadcasted_iota(jnp.int32, (1, LANES), 1)
    keep_odd = lane < tiles - 1

    def work(source, target, index=0):
        totals = [jnp.zeros((channels, 2 * channels), jnp.float32)] * NMOM
        done = 0

        def catch_up(goal):
            nonlocal done
            while source is not None and done < min(goal, lines):
                add_cross(channels, keep_odd, *slots[source], done, totals)
                done += 1

        if target is not None:
            for tile in range(tiles):
                spread_samples(strain.at[index : index + 1], xs, tile)
            for pair in range(pairs):
                transform(table, xs, *slots[target], pair)
                catch_up((pair + 1) * lines // pairs)
        catch_up(lines)
        if source is None:
            return
        block = 2 * step_index + index - 1
        for moment in range(NMOM):
            whole = (totals[moment][:, :channels] + totals[moment][:, channels:]) * (1.0 / SEGLEN)
            gap = jnp.zeros((channels, CPAD - channels), jnp.float32)
            high, middle, low = split3(jnp.concatenate([whole, gap] * 2, axis=1))
            start = pl.multiple_of((moment * blocks + block) * channels, 16)
            parts[pl.ds(start, channels), :LANES] = jnp.where(lane < CPAD, high, middle)
            parts[pl.ds(start, channels), LANES:] = low

    @pl.when(step_index == 0)
    def _():
        xs[tiles * STRIDE :, :] = jnp.zeros((xs.shape[0] - tiles * STRIDE, LANES), jnp.float32)
        weights[...] = jnp.zeros_like(weights)
        for part in range(3):
            weights[part * CPAD : part * CPAD + channels, :] = influence[...]
        work(None, 0, 0)
        work(0, 1, 1)

    @pl.when(step_index > 0)
    def _():
        work(1, 0, 0)
        work(0, 1, 1)

    @pl.when(step_index == blocks // 2 - 1)
    def _():
        work(1, None, 2)
        width = 2 * LANES
        count = hotspots // width
        part = out.shape[0] // (hotspots // LANES)
        for first in range(0, count, GROUP):
            values = []
            for moment in range(NMOM):
                rows = slice(moment * blocks * channels, (moment + 1) * blocks * channels)
                values.append([])
                for step in range(first, first + GROUP):
                    lanes = slice(step * width, (step + 1) * width)
                    column = influence[:, lanes].astype(jnp.float32)
                    spread = jnp.dot(parts[rows, :], weights[:, lanes], preferred_element_type=jnp.float32)
                    spread = spread.reshape(blocks, channels, width)
                    values[-1].append(jnp.sum(spread * column[None], axis=1))
            values = [jnp.concatenate(value, axis=1) for value in values]
            if damages:
                values = [dirlik(*values)]
            for half in range(2 * GROUP):
                start = (2 * first + half) * part
                for value in values:
                    out[start : start + blocks, :] = value[:, half * LANES : (half + 1) * LANES]
                    start += blocks
        named = jnp.zeros((1, LANES), jnp.float32)
        for index in range(blocks):
            label = (labels[0, index] * NDIR + labels[1, index]) * NYAW + labels[2, index]
            named = jnp.where(lane % blocks == index, label.astype(jnp.float32), named)
        for step in range(hotspots // LANES):
            out[(step + 1) * part - 1 : (step + 1) * part, :] = named


def local_rows(strain, bin_labels, influence, damages):
    blocks, channels, samples = strain.shape
    hotspots = influence.shape[0]
    tiles = samples // LANES
    rows = ((1 if damages else NMOM) * blocks + 1) * (hotspots // LANES)
    return pl.pallas_call(
        functools.partial(moments_kernel, blocks, channels, tiles, damages),
        grid=(blocks // 2,),
        in_specs=[
            pl.BlockSpec(memory_space=pltpu.SMEM),
            pl.BlockSpec((2, channels, samples), lambda b: (b, 0, 0)),
            pl.BlockSpec((2 * SEGLEN, 2 * SEGLEN), lambda b: (0, 0)),
            pl.BlockSpec((channels, hotspots), lambda b: (0, 0)),
        ],
        out_specs=pl.BlockSpec((rows, LANES), lambda b: (0, 0)),
        out_shape=jax.ShapeDtypeStruct((rows, LANES), jnp.float32),
        scratch_shapes=[
            pltpu.VMEM(((WINDOWS + 1) * STRIDE, LANES), jnp.float32),
            *[pltpu.VMEM((SEGLEN * STRIDE, LANES), jnp.float32)] * 4,
            pltpu.VMEM((2 * LANES, hotspots), jnp.bfloat16),
            pltpu.VMEM((NMOM * blocks * channels, 2 * LANES), jnp.bfloat16),
        ],
        compiler_params=pltpu.CompilerParams(vmem_limit_bytes=60 << 20),
        name="block_moments",
    )(bin_labels.T, strain, jnp.asarray(pair_table()), influence.T)


def dirlik(moment_zero, moment_one, moment_two, moment_four):
    spread_ratio = moment_two / jnp.sqrt(moment_zero * moment_four)
    mean_freq = moment_one / moment_zero * jnp.sqrt(moment_two / moment_four)
    d_one = 2.0 * (mean_freq - spread_ratio**2) / (1.0 + spread_ratio**2)
    shared = 1.0 - spread_ratio - d_one + d_one**2
    r_ratio = (spread_ratio - mean_freq - d_one**2) / shared
    d_two = shared / (1.0 - r_ratio)
    d_three = 1.0 - d_one - d_two
    q_factor = 1.25 * (spread_ratio - d_three - d_two * r_ratio) / d_one
    peak_rate = jnp.sqrt(moment_four / moment_two)
    bracket = 6.0 * d_one * q_factor**3 + 2.8284271247 * 1.3293403882 * (
        jnp.abs(r_ratio) ** 3 * d_two + d_three
    )
    return peak_rate * (2.0 * jnp.sqrt(moment_zero)) ** 3 * bracket


def gather_kernel(sources, received, damage, total):
    count_blocks, width = damage.shape
    blocks = count_blocks // sources
    part = blocks + 1
    by_block = jnp.concatenate(
        [received[source * part : source * part + blocks, :] for source in range(sources)], axis=0
    )
    named = jnp.concatenate(
        [received[(source + 1) * part - 1 : (source + 1) * part, :] for source in range(sources)], axis=0
    )
    source = lax.broadcasted_iota(jnp.int32, named.shape, 0)
    lane = lax.broadcasted_iota(jnp.int32, named.shape, 1)
    named = jnp.sum(jnp.where(lane // blocks == source, named, 0.0), axis=0, keepdims=True)
    bins = lax.broadcasted_iota(jnp.int32, (NBIN, count_blocks), 0).astype(jnp.float32)
    chosen = jnp.where(named == bins, 1.0, 0.0).astype(jnp.bfloat16)
    by_bin = jnp.zeros((NBIN, width), jnp.float32)
    for piece in split3(by_block):
        by_bin = by_bin + jnp.dot(chosen, piece, preferred_element_type=jnp.float32)
    damage[...] = by_bin
    total[...] = jnp.sum(by_block * (1.0 / count_blocks), axis=0, keepdims=True)


def bin_kernel(named, moments, damage, total):
    count_blocks = named.shape[1]
    bins = lax.broadcasted_iota(jnp.int32, (NBIN, count_blocks), 0).astype(jnp.float32)
    member = jnp.where(named[...] == bins, 1.0, 0.0)
    count = jnp.sum(member, axis=1, keepdims=True)
    chosen = member.astype(jnp.bfloat16)
    means = []
    for moment in range(NMOM):
        total_moment = jnp.zeros(damage.shape, jnp.float32)
        for piece in split3(moments[moment]):
            total_moment = total_moment + jnp.dot(chosen, piece, preferred_element_type=jnp.float32)
        means.append(total_moment / count)
    by_bin = dirlik(*means)
    damage[...] = by_bin
    total[...] = jnp.sum(count / count_blocks * by_bin, axis=0, keepdims=True)


def per_device(strain, bin_labels, influence):
    devices = lax.axis_size("tm")
    blocks = strain.shape[0]
    hotspots = influence.shape[0]
    width = hotspots // devices
    out_shape = (
        jax.ShapeDtypeStruct((NBIN, width), jnp.float32),
        jax.ShapeDtypeStruct((1, width), jnp.float32),
    )
    if blocks * devices == NBIN and width == LANES:
        rows = local_rows(strain, bin_labels, influence, True)
        rows = rows.reshape(devices, 1, (blocks + 1) * LANES)
        received = lax.all_to_all(rows, "tm", split_axis=0, concat_axis=0, tiled=True)
        damage, total = pl.pallas_call(
            functools.partial(gather_kernel, devices), out_shape=out_shape, name="gather_damage"
        )(received.reshape(devices * (blocks + 1), LANES))
        return damage, total.reshape(width)
    rows = local_rows(strain, bin_labels, influence, False)
    rows = rows.reshape(hotspots // LANES, NMOM * blocks + 1, LANES)
    named = jnp.broadcast_to(rows[:1, -1, :blocks], (devices, blocks))
    moments = rows[:, :-1].reshape(hotspots // LANES, NMOM, blocks, LANES)
    moments = moments.transpose(1, 2, 0, 3).reshape(NMOM, blocks, devices, width)
    moments = moments.transpose(2, 0, 1, 3).reshape(devices, NMOM * blocks * width)
    sent = jnp.concatenate([moments, named], axis=1)
    received = lax.all_to_all(sent, "tm", split_axis=0, concat_axis=0, tiled=True)
    named = received[:, -blocks:].reshape(1, devices * blocks)
    moments = received[:, :-blocks].reshape(devices, NMOM, blocks, width)
    moments = moments.transpose(1, 0, 2, 3).reshape(NMOM, devices * blocks, width)
    damage, total = pl.pallas_call(bin_kernel, out_shape=out_shape, name="bin_damage")(named, moments)
    return damage, total.reshape(width)


def solution(mesh):
    placed = (P(("groups", "tm"), None, None), P(("groups", "tm"), None), P())
    return jax.shard_map(
        per_device,
        mesh=mesh,
        in_specs=placed,
        out_specs=(P("groups", "tm"), P(("groups", "tm"))),
        check_vma=False,
    )
```
